32 devices in a mesh: grp: 4 (over x, core), row: 2 (over y), col: 4 (over z).
Axes of the slice: x: 2, y: 2, z: 4, core: 2. Of those that a mesh axis runs over, the one named last changes fastest.
Arguments:
- density: bfloat16 [256, 15, 128, 128], P(('grp', 'row', 'col')), may hold values from -0.29882812 to 0.29882812
- block_mask: int32 [256, 15], P(('grp', 'row', 'col')), may hold values 0 or 1
- orbital_cell: int32 [32768], P(('grp', 'row', 'col')), may hold values from 0 to 16383
- slab_of_device: int32 [32], replicated, may hold values from 0 to 31, each once
- positions: float32 [3, 16384], P(None, ('grp', 'row', 'col')), may hold values from 0 to 1
- charges: float32 [16384], P(('grp', 'row', 'col')), may hold values from -3 to 3
Outputs:
- new_density: bfloat16 [256, 15, 128, 128], P(('grp', 'row', 'col'))
- energies: float32 [16384], P(('grp', 'row', 'col'))
The draws below stay inside these ranges and needn't reach their ends.
Inputs may be any that keep to these rules, and one draw needn't show every extreme that they name: `orbital_cell`: cell numbers lie within one slab of 1 planes. `slab_of_device`: a permutation of the slabs.
All inputs are finite; a program needn't handle non-finite values. No bound on the sum of `block_mask` on one device may be relied on, other than what follows from the above.
Results may differ from the reference program's by a relative error of at most 0.0031.
Values may be sent and summed in bfloat16 or wider, within the bound.
No kernel may reach another device: no remote copies, remote signals or barrier semaphores. Data moves between devices by JAX's collectives and lax.ppermute only.
A program may use at most 128 MiB of HBM per device.

```python
import jax
import jax.numpy as jnp
from jax import lax

BS = 128
BAND = 7
SLOTS = 15
ROWS_DEV = 8
NBLOCKS = 256
ORBITALS = 32768
PLANES_DEV = 1
GRID_Y = 128
GRID_Z = 128
GRID_X = 32
ATOMS = 16384
N_GRP = 4
N_ROW = 2
N_COL = 4


def with_ends(drawn, stream_key, smallest, largest):
    shape = drawn.shape
    place = [jax.random.randint(jax.random.fold_in(stream_key, axis), (), 0, shape[axis]) for axis in range(len(shape))]
    drawn = drawn.at[tuple(place)].set(smallest)
    longest = shape.index(max(shape))
    place[longest] = (place[longest] + 1) % shape[longest]
    return drawn.at[tuple(place)].set(largest)


def level_of(rng, extent, pieces, least, high):
    gain = 1.0
    for position, shards_of in pieces:
        steps = jax.random.uniform(jax.random.fold_in(jax.random.fold_in(rng, 6), position), (shards_of,), jnp.float32, least / len(pieces), high / len(pieces))
        gain = gain * jnp.repeat(jnp.exp(steps), extent[position] // shards_of).reshape((-1,) + (1,) * (len(extent) - 1 - position))
    return gain


def noise(stream_key, shape, deviation, reach, shards=(), held_as=jnp.bfloat16):
    factor_of = level_of(stream_key, shape, shards, -0.22, 0.18) if shards else 1.0
    entries = jax.random.normal(stream_key, shape, jnp.float32) * deviation * factor_of
    return jnp.minimum(jnp.maximum(entries, -reach), reach).astype(held_as)


def setup_inputs(seed: int = 0) -> dict:
    streams_of = jax.random.split(jax.random.key(seed), 7)
    density = noise(streams_of[0], (NBLOCKS, SLOTS, BS, BS), 0.05, 0.29882812, ((0, 32),))
    block_mask = with_ends((jax.random.randint(streams_of[1], (NBLOCKS, SLOTS), 0, 4) < 3).astype(jnp.int32), jax.random.fold_in(streams_of[1], 1), 0, 1)
    orbital_cell = with_ends(jax.random.randint(streams_of[2], (ORBITALS,), 0, PLANES_DEV * GRID_Y * GRID_Z), jax.random.fold_in(streams_of[2], 1), 0, (PLANES_DEV * GRID_Y * GRID_Z) - 1).astype(jnp.int32)
    slab_of_device = jax.random.permutation(streams_of[3], N_GRP * N_ROW * N_COL).astype(jnp.int32)
    positions = jnp.clip(1.0 * jax.random.uniform(streams_of[4], (3, ATOMS), jnp.float32) ** level_of(streams_of[4], (3, ATOMS), ((1, 32),), -0.2, 0.2), 0.0, 1.0)
    charges = noise(streams_of[5], (ATOMS,), 0.5, 3.0, ((0, 32),), jnp.float32)
    return dict(density=density, block_mask=block_mask, orbital_cell=orbital_cell, slab_of_device=slab_of_device, positions=positions, charges=charges)


SPREAD = 2.0
COUPLE = 0.5
DENSITY_SCALE = 0.05


def gaussian(centre, points):
    offset = points[:, None] - centre[None, :]
    return jnp.exp(-offset * offset / (2.0 * SPREAD * SPREAD))


def atom_tables(positions, grid_x):
    height = jnp.arange(GRID_Y, dtype=jnp.float32)
    depth = jnp.arange(GRID_Z, dtype=jnp.float32)
    return positions[0] * grid_x, gaussian(positions[1] * GRID_Y, height), gaussian(positions[2] * GRID_Z, depth)


def plane_potential(plane_id, xcoord, along_y, along_z, charges):
    weight = gaussian(xcoord, plane_id.astype(jnp.float32)[None])[0] * charges
    return jnp.dot(along_y * weight[None, :], along_z.T, precision=lax.Precision.HIGHEST)


def plane_energy(rho_plane, plane_id, xcoord, along_y, along_z):
    weight = gaussian(xcoord, plane_id.astype(jnp.float32)[None])[0]
    inner_sum = jnp.dot(rho_plane, along_z, precision=lax.Precision.HIGHEST)
    return weight * jnp.sum(inner_sum * along_y, axis=0)


def make_work(density, valid_blocks, shifts):
    masked = density * valid_blocks.astype(jnp.bfloat16)[:, :, None, None]
    identity = jnp.eye(BS, dtype=jnp.float32)
    centre_block = (density[:, BAND].astype(jnp.float32) - shifts[:, :, None] * identity[None]) * valid_blocks[:, BAND][:, None, None]
    return masked.at[:, BAND].set(centre_block.astype(jnp.bfloat16))


def band_square(padded, number):
    results = []
    for slot in range(SLOTS):
        lowest = max(0, slot - BAND)
        highest = min(SLOTS - 1, slot + BAND)
        left_side = padded[BAND:BAND + number, lowest:highest + 1].astype(jnp.float32)
        right_side = jnp.stack([padded[shift_id:shift_id + number, slot - shift_id + BAND] for shift_id in range(lowest, highest + 1)], axis=1).astype(jnp.float32)
        results.append(jnp.einsum("raij,rajk->rik", left_side, right_side))
    return jnp.stack(results, axis=1)


def reference(density, block_mask, orbital_cell, slab_of_device, positions, charges):
    members = NBLOCKS // ROWS_DEV
    xcoord, along_y, along_z = atom_tables(positions, GRID_X)
    plane_ids = jnp.arange(GRID_X, dtype=jnp.int32)
    potential = lax.map(lambda plane_id: plane_potential(plane_id, xcoord, along_y, along_z, charges), plane_ids)
    cells_here = PLANES_DEV * GRID_Y * GRID_Z
    orbital_ids = jnp.arange(ORBITALS, dtype=jnp.int32)
    owners = orbital_ids // (ROWS_DEV * BS)
    global_cell = (slab_of_device[owners] * cells_here + orbital_cell).astype(jnp.int32)
    shifts = (COUPLE * potential.reshape(-1)[global_cell]).reshape(NBLOCKS, BS)
    row_ids = jnp.arange(NBLOCKS, dtype=jnp.int32)
    columns = row_ids[:, None] + jnp.arange(SLOTS, dtype=jnp.int32)[None, :] - BAND
    inside = ((columns >= 0) & (columns < NBLOCKS)).astype(jnp.int32)
    valid_blocks = (block_mask * inside).astype(jnp.float32)
    padded_density = jnp.pad(density, ((BAND, BAND), (0, 0), (0, 0), (0, 0)))
    padded_valid = jnp.pad(valid_blocks, ((BAND, BAND), (0, 0)))
    padded_shift = jnp.pad(shifts, ((BAND, BAND), (0, 0)))

    def one_panel(panel):
        offset = (panel * ROWS_DEV).astype(jnp.int32)
        rows_density = lax.dynamic_slice_in_dim(padded_density, offset, ROWS_DEV + 2 * BAND, 0)
        rows_valid = lax.dynamic_slice_in_dim(padded_valid, offset, ROWS_DEV + 2 * BAND, 0)
        rows_shift = lax.dynamic_slice_in_dim(padded_shift, offset, ROWS_DEV + 2 * BAND, 0)
        work = make_work(rows_density, rows_valid, rows_shift)
        squared = band_square(work, ROWS_DEV)
        own = work[BAND:BAND + ROWS_DEV].astype(jnp.float32)
        panel_valid = rows_valid[BAND:BAND + ROWS_DEV]
        return (panel_valid[:, :, None, None] * (2.0 * own - squared)).astype(jnp.bfloat16)

    new_density = lax.map(one_panel, jnp.arange(members, dtype=jnp.int32)).reshape(NBLOCKS, SLOTS, BS, BS)
    diagonal_values = jnp.diagonal(new_density[:, BAND], axis1=1, axis2=2).astype(jnp.float32).reshape(-1) * DENSITY_SCALE
    grid_density = jnp.zeros((GRID_X * GRID_Y * GRID_Z,), jnp.float32).at[global_cell].add(diagonal_values)
    grid_density = grid_density.reshape(GRID_X, GRID_Y, GRID_Z)

    def add_plane(running, plane_id):
        return running + plane_energy(grid_density[plane_id], plane_id, xcoord, along_y, along_z), None

    summed, unused = lax.scan(add_plane, jnp.zeros((ATOMS,), jnp.float32), plane_ids)
    return new_density, charges * summed
```

```python
import functools

import jax
import jax.numpy as jnp
from jax import lax
from jax.experimental import pallas as pl
from jax.experimental.pallas import tpu as pltpu
from jax.sharding import PartitionSpec as P

BS = 128
BAND = 7
SLOTS = 15
PLANES_DEV = 1
GRID_Y = 128
GRID_Z = 128

SPREAD = 2.0
COUPLE = 0.5
DENSITY_SCALE = 0.05

AX = ("grp", "row", "col")
ROWS = 8
EXT = ROWS + 2 * BAND

NEXT_CHUNKS = ((7, 6), (5, 4, 3, 2, 1))
PREV_CHUNKS = ((0, 1), (2, 3, 4, 5, 6))


def next_blocks(rows):
    return [(r, c) for r in rows for c in range(ROWS, r + BAND + 1)]


def prev_blocks(rows):
    return [(r, c) for r in rows for c in range(r - BAND, 0)]


def runs(rows, blocks_of):
    place = 0
    for r in rows:
        blocks = blocks_of((r,))
        yield r, blocks[0][1] - r + BAND, len(blocks), place
        place += len(blocks)


def valid_at(info, mask, r, s):
    row = info[0] * ROWS + r
    column = row + s - BAND
    inside = jnp.logical_and(column >= 0, column < info[1] * ROWS)
    return jnp.where(inside, mask[r, s], 0)


VMEM = pl.BlockSpec(memory_space=pltpu.VMEM)
SMEM = pl.BlockSpec(memory_space=pltpu.SMEM)
ANY = pl.BlockSpec(memory_space=pl.ANY)


def cost(flops, nbytes, exps=0):
    return pl.CostEstimate(flops=int(flops), bytes_accessed=int(nbytes), transcendentals=int(exps))


def pack_kernel(info, mask, density, *refs):
    nchunk = len(NEXT_CHUNKS)
    outs, (scratch, sems) = refs[: 2 * nchunk], refs[2 * nchunk :]
    jobs = []
    for c in range(nchunk):
        for out, rows, blocks_of in (
            (outs[2 * c], PREV_CHUNKS[c], prev_blocks),
            (outs[2 * c + 1], NEXT_CHUNKS[c], next_blocks),
        ):
            for r, s, count, place in runs(rows, blocks_of):
                jobs.append((out, r, s, count, place))
    copies = []
    base = 0
    for j, (out, r, s, count, place) in enumerate(jobs):
        copy = pltpu.make_async_copy(
            density.at[r, pl.ds(s, count)], scratch.at[pl.ds(base, count)], sems.at[j]
        )
        copy.start()
        copies.append((copy, base))
        base += count
    for (out, r, s, count, place), (copy, start) in zip(jobs, copies):
        copy.wait()
        for b in range(count):
            keep = valid_at(info, mask, r, s + b).astype(jnp.float32).astype(jnp.bfloat16)
            out[place + b] = scratch[start + b] * keep


def pack(info, mask, density):
    shapes = []
    for c in range(len(NEXT_CHUNKS)):
        for blocks in (prev_blocks(PREV_CHUNKS[c]), next_blocks(NEXT_CHUNKS[c])):
            shapes.append(jax.ShapeDtypeStruct((len(blocks), BS, BS), jnp.bfloat16))
    total = sum(s.shape[0] for s in shapes)
    return pl.pallas_call(
        pack_kernel,
        out_shape=shapes,
        in_specs=[SMEM, SMEM, ANY],
        out_specs=[VMEM] * len(shapes),
        scratch_shapes=[
            pltpu.VMEM((total, BS, BS), jnp.bfloat16),
            pltpu.SemaphoreType.DMA((2 * BAND,)),
        ],
        cost_estimate=cost(total * BS * BS, 4 * total * BS * BS),
        name="pack",
    )(info, mask, density)


def split(x):
    high = x.astype(jnp.bfloat16)
    return high, (x - high.astype(jnp.float32)).astype(jnp.bfloat16)


def table(centre, points):
    offset = points - centre
    return jnp.exp(offset * offset * (-1.0 / (2.0 * SPREAD * SPREAD)))


def grid_points(lanes):
    return lax.broadcasted_iota(jnp.int32, (GRID_Y, lanes), 0).astype(jnp.float32)


def plane_of(info):
    return (info[2] * PLANES_DEV).astype(jnp.float32)


def shift_kernel(info, atoms, cell, shifts):
    members = atoms.shape[0]
    lanes = atoms.shape[2]
    plane = plane_of(info)
    grid_x = (info[1] * PLANES_DEV).astype(jnp.float32)
    points = grid_points(lanes)

    def step(i, total):
        part = atoms[i]
        weight = table(part[0:1] * grid_x, plane) * part[3:4]
        along_y = table(part[1:2] * GRID_Y, points) * weight
        along_z = table(part[2:3] * GRID_Z, points)
        y_high, y_low = split(along_y)
        z_high, z_low = split(along_z)
        return total + lax.dot_general(
            jnp.concatenate([z_high, z_low], axis=0),
            jnp.concatenate([y_high, y_low], axis=0),
            (((1,), (1,)), ((), ())),
            preferred_element_type=jnp.float32,
        )

    total = lax.fori_loop(0, members, step, jnp.zeros((2 * GRID_Z, 2 * GRID_Y), jnp.float32))
    potential = (
        total[:GRID_Z, :GRID_Y]
        + (total[:GRID_Z, GRID_Y:] + total[GRID_Z:, :GRID_Y])
        + total[GRID_Z:, GRID_Y:]
    )
    high, rest = split(potential)
    middle, low = split(potential - high.astype(jnp.float32))
    cells = cell[...]
    orbitals = cells.shape[1]
    ids = lax.broadcasted_iota(jnp.int32, (GRID_Y, orbitals), 0)
    at_y = (ids == cells // GRID_Z).astype(jnp.float32).astype(jnp.bfloat16)
    stacked = jnp.concatenate([high, middle, low], axis=0)
    picked = jnp.dot(stacked, at_y, preferred_element_type=jnp.float32)
    picked = picked[:GRID_Z] + (picked[GRID_Z : 2 * GRID_Z] + picked[2 * GRID_Z :])
    here = jnp.where(ids == cells % GRID_Z, picked, 0.0)
    shifts[...] = COUPLE * jnp.sum(here, axis=0, keepdims=True)


def shift_values(info, atoms, cell):
    members, _, lanes = atoms.shape
    return pl.pallas_call(
        shift_kernel,
        out_shape=jax.ShapeDtypeStruct(cell.shape, jnp.float32),
        in_specs=[SMEM, VMEM, VMEM],
        out_specs=VMEM,
        cost_estimate=cost(
            2 * 4 * GRID_Y * GRID_Z * members * lanes, 16 * members * lanes, 2 * GRID_Y * members * lanes
        ),
        name="shifts",
    )(info, atoms, cell)


def eye():
    return lax.broadcasted_iota(jnp.int32, (BS, BS), 0) == lax.broadcasted_iota(jnp.int32, (BS, BS), 1)


def work_kernel(info, mask, shifts, density, out):
    diagonal = eye()
    for r in range(ROWS):
        for p in range(EXT):
            s = p - r
            rows, columns = slice(r * BS, (r + 1) * BS), slice(p * BS, (p + 1) * BS)
            if s < 0 or s >= SLOTS:
                out[rows, columns] = jnp.zeros((BS, BS), jnp.bfloat16)
                continue
            keep = valid_at(info, mask, r, s).astype(jnp.float32)
            if s == BAND:
                shift = jnp.where(diagonal, shifts[0:1, rows], 0.0)
                out[rows, columns] = ((density[r, s].astype(jnp.float32) - shift) * keep).astype(jnp.bfloat16)
            else:
                out[rows, columns] = density[r, s] * keep.astype(jnp.bfloat16)


def work_matrix(info, mask, shifts, density):
    return pl.pallas_call(
        work_kernel,
        out_shape=jax.ShapeDtypeStruct((ROWS * BS, EXT * BS), jnp.bfloat16),
        in_specs=[SMEM, SMEM, VMEM, VMEM],
        out_specs=VMEM,
        cost_estimate=cost(ROWS * SLOTS * BS * BS, 4 * ROWS * EXT * BS * BS),
        name="work",
    )(info, mask, shifts, density)


def mine(first, last):
    return slice((first + BAND) * BS, (last + BAND) * BS)


def groups(rows):
    return [rows[i : i + 2] for i in range(0, len(rows), 2)]


def partial_kernel(chunk, work, above, below, to_prev, to_next, strip):
    for packed, out, rows, blocks_of, down in (
        (above, to_prev, NEXT_CHUNKS[chunk], next_blocks, True),
        (below, to_next, PREV_CHUNKS[chunk], prev_blocks, False),
    ):
        places = {r: (count, place) for r, _, count, place in runs(rows, blocks_of)}
        for group in groups(rows):
            width = max(places[r][0] for r in group)
            for g, r in enumerate(group):
                count, place = places[r]
                pad = 0 if down else width - count
                for b in range(width):
                    inside = pad <= b < pad + count
                    strip[g * BS : (g + 1) * BS, b * BS : (b + 1) * BS] = (
                        packed[place + b - pad] if inside else jnp.zeros((BS, BS), jnp.bfloat16)
                    )
            first, last = (0, width) if down else (ROWS - width, ROWS)
            product = jnp.dot(
                strip[: len(group) * BS, : width * BS],
                work[first * BS : last * BS, mine(first, last)],
                preferred_element_type=jnp.float32,
            ).astype(jnp.bfloat16)
            for g, r in enumerate(group):
                count, place = places[r]
                pad = 0 if down else width - count
                for b in range(count):
                    out[place + b] = product[g * BS : (g + 1) * BS, (pad + b) * BS : (pad + b + 1) * BS]


def partial_products(chunk, work, above, below):
    n_next, n_prev = above.shape[0], below.shape[0]
    return pl.pallas_call(
        functools.partial(partial_kernel, chunk),
        out_shape=[
            jax.ShapeDtypeStruct(above.shape, jnp.bfloat16),
            jax.ShapeDtypeStruct(below.shape, jnp.bfloat16),
        ],
        in_specs=[VMEM, VMEM, VMEM],
        out_specs=[VMEM, VMEM],
        scratch_shapes=[pltpu.VMEM((2 * BS, BAND * BS), jnp.bfloat16)],
        cost_estimate=cost(2 * 5 * (n_next + n_prev) * BS**3, 4 * ROWS * EXT * BS * BS),
        name=f"partial{chunk}",
    )(work, above, below)


def own_kernel(info, mask, work, *refs):
    nchunk = len(NEXT_CHUNKS)
    received = refs[: 2 * nchunk]
    out, diagonal_out, right, result, sems = refs[2 * nchunk :]
    size = ROWS * BS
    right[: BAND * BS] = jnp.zeros((BAND * BS, size), jnp.bfloat16)
    right[(BAND + ROWS) * BS :] = jnp.zeros((BAND * BS, size), jnp.bfloat16)
    right[BAND * BS : (BAND + ROWS) * BS] = work[:, mine(0, ROWS)]
    for c in range(nchunk):
        above, below = received[2 * c], received[2 * c + 1]
        for b, (r, column) in enumerate(next_blocks(NEXT_CHUNKS[c])):
            k, j = r - ROWS + BAND, column - ROWS
            right[k * BS : (k + 1) * BS, j * BS : (j + 1) * BS] = above[b]
        for b, (r, column) in enumerate(prev_blocks(PREV_CHUNKS[c])):
            k, j = r + ROWS + BAND, column + ROWS
            right[k * BS : (k + 1) * BS, j * BS : (j + 1) * BS] = below[b]
    on_diagonal = eye()
    copies = []
    for pair in range(ROWS // 2):
        first = 2 * pair
        squared = jnp.dot(
            work[first * BS : (first + 2) * BS, first * BS : (first + 16) * BS],
            right[first * BS : (first + 16) * BS, :],
            preferred_element_type=jnp.float32,
        )
        for g in range(2):
            r = first + g
            for j in range(ROWS):
                keep = valid_at(info, mask, r, j - r + BAND).astype(jnp.float32)
                mine_now = work[r * BS : (r + 1) * BS, mine(j, j + 1)].astype(jnp.float32)
                value = keep * (2.0 * mine_now - squared[g * BS : (g + 1) * BS, j * BS : (j + 1) * BS])
                value = value.astype(jnp.bfloat16)
                result[r, j] = value
                if j == r:
                    kept = jnp.where(on_diagonal, value.astype(jnp.float32), 0.0)
                    diagonal_out[0:1, r * BS : (r + 1) * BS] = jnp.sum(kept, axis=0, keepdims=True)
            copy = pltpu.make_async_copy(result.at[r], out.at[r, pl.ds(BAND - r, ROWS)], sems.at[r])
            copy.start()
            copies.append(copy)
    for copy in copies:
        copy.wait()


def own_products(info, mask, work, received, shape):
    size = ROWS * BS
    return pl.pallas_call(
        own_kernel,
        out_shape=[
            jax.ShapeDtypeStruct(shape, jnp.bfloat16),
            jax.ShapeDtypeStruct((1, size), jnp.float32),
        ],
        in_specs=[SMEM, SMEM, VMEM] + [VMEM] * len(received),
        out_specs=[ANY, VMEM],
        scratch_shapes=[
            pltpu.VMEM((EXT * BS, size), jnp.bfloat16),
            pltpu.VMEM((ROWS, ROWS, BS, BS), jnp.bfloat16),
            pltpu.SemaphoreType.DMA((ROWS,)),
        ],
        cost_estimate=cost(2 * size * size * 2048, 4 * size * EXT * BS),
        name="own",
    )(info, mask, work, *received)


def side_kernel(work, to_next, to_prev):
    nxt = {b: i for i, b in enumerate(next_blocks(range(1, ROWS)))}
    prv = {b: i for i, b in enumerate(prev_blocks(range(ROWS - 1)))}
    for pair in range(ROWS // 2):
        first = 2 * pair
        rows = slice(first * BS, (first + 2) * BS)
        for places, out, lo, hi, k0, k1 in (
            (nxt, to_next, ROWS, first + 1 + BAND + 1, 1, ROWS),
            (prv, to_prev, first - BAND, 0, 0, ROWS - 1),
        ):
            squared = jnp.dot(
                work[rows, mine(k0, k1)],
                work[k0 * BS : k1 * BS, mine(lo, hi)],
                preferred_element_type=jnp.float32,
            )
            for g in range(2):
                r = first + g
                for c in range(lo, hi):
                    if (r, c) not in places:
                        continue
                    own = work[r * BS : (r + 1) * BS, mine(c, c + 1)].astype(jnp.float32)
                    out[places[r, c]] = (
                        2.0 * own - squared[g * BS : (g + 1) * BS, (c - lo) * BS : (c - lo + 1) * BS]
                    )


def side_products(work):
    count = BAND * (BAND + 1) // 2
    shape = jax.ShapeDtypeStruct((count, BS, BS), jnp.float32)
    return pl.pallas_call(
        side_kernel,
        out_shape=[shape, shape],
        in_specs=[VMEM],
        out_specs=[VMEM, VMEM],
        cost_estimate=cost(2 * 9 * count * BS**3, 4 * ROWS * BS * EXT * BS),
        name="side",
    )(work)


def finish_kernel(info, mask, at_next, at_prev, *refs):
    nchunk = len(NEXT_CHUNKS)
    received = refs[: 2 * nchunk]
    _, out, result, sems = refs[2 * nchunk :]
    nxt = {b: i for i, b in enumerate(next_blocks(range(1, ROWS)))}
    prv = {b: i for i, b in enumerate(prev_blocks(range(ROWS - 1)))}
    copies = []
    base = 0
    for c in range(nchunk):
        for packed, local, places, rows, blocks_of in (
            (received[2 * c], at_next, nxt, NEXT_CHUNKS[c], next_blocks),
            (received[2 * c + 1], at_prev, prv, PREV_CHUNKS[c], prev_blocks),
        ):
            for r, s, count, place in runs(rows, blocks_of):
                for b in range(count):
                    keep = valid_at(info, mask, r, s + b).astype(jnp.float32)
                    value = local[places[r, s + b + r - BAND]] - packed[place + b].astype(jnp.float32)
                    result[base + b] = (keep * value).astype(jnp.bfloat16)
                copy = pltpu.make_async_copy(
                    result.at[pl.ds(base, count)], out.at[r, pl.ds(s, count)], sems.at[len(copies)]
                )
                copy.start()
                copies.append(copy)
                base += count
    for copy in copies:
        copy.wait()


def finish(info, mask, at_next, at_prev, received, new_density):
    count = BAND * (BAND + 1)
    operands = [info, mask, at_next, at_prev, *received, new_density]
    return pl.pallas_call(
        finish_kernel,
        out_shape=jax.ShapeDtypeStruct(new_density.shape, new_density.dtype),
        in_specs=[SMEM, SMEM] + [VMEM] * (2 + len(received)) + [ANY],
        out_specs=ANY,
        scratch_shapes=[
            pltpu.VMEM((count, BS, BS), jnp.bfloat16),
            pltpu.SemaphoreType.DMA((2 * BAND,)),
        ],
        input_output_aliases={len(operands) - 1: 0},
        cost_estimate=cost(3 * count * BS * BS, 8 * count * BS * BS),
        name="finish",
    )(*operands)


def energy_kernel(info, atoms, cell, diagonal, out):
    members = atoms.shape[0]
    lanes = atoms.shape[2]
    plane = plane_of(info)
    grid_x = (info[1] * PLANES_DEV).astype(jnp.float32)
    points = grid_points(lanes)
    cells = cell[...]
    ids = lax.broadcasted_iota(jnp.int32, (GRID_Y, cells.shape[1]), 0)
    at_y = jnp.where(ids == cells // GRID_Z, diagonal[...], 0.0).astype(jnp.bfloat16)
    at_z = (ids == cells % GRID_Z).astype(jnp.float32).astype(jnp.bfloat16)
    rho = lax.dot_general(
        at_y, at_z, (((1,), (1,)), ((), ())), preferred_element_type=jnp.float32
    )
    high, low = split(rho * DENSITY_SCALE)
    rho_wide = jnp.concatenate([high, high], axis=1)

    def step(i, carry):
        part = atoms[i]
        weight = table(part[0:1] * grid_x, plane)
        along_y = table(part[1:2] * GRID_Y, points)
        z_high, z_low = split(table(part[2:3] * GRID_Z, points))
        inner = jnp.dot(
            rho_wide, jnp.concatenate([z_high, z_low], axis=0), preferred_element_type=jnp.float32
        ) + jnp.dot(low, z_high, preferred_element_type=jnp.float32)
        energy = jnp.sum(inner * along_y, axis=0, keepdims=True) * weight
        for q in range(lanes // BS):
            out[i, q : q + 1, :] = energy[:, q * BS : (q + 1) * BS]
        return carry

    lax.fori_loop(0, members, step, 0)


def energy_shares(info, atoms, cell, diagonal):
    members, _, lanes = atoms.shape
    return pl.pallas_call(
        energy_kernel,
        out_shape=jax.ShapeDtypeStruct((members, lanes // BS, BS), jnp.float32),
        in_specs=[SMEM, VMEM, VMEM, VMEM],
        out_specs=VMEM,
        cost_estimate=cost(
            2 * 3 * GRID_Y * GRID_Z * members * lanes, 16 * members * lanes, 2 * GRID_Y * members * lanes
        ),
        name="energy",
    )(info, atoms, cell, diagonal)


def on_device(density, block_mask, orbital_cell, slab_of_device, positions, charges):
    members = lax.axis_size(AX)
    my_index = lax.axis_index(AX)
    info = jnp.stack([my_index, jnp.int32(members), slab_of_device[my_index]]).astype(jnp.int32)
    forward = [(i, i + 1) for i in range(members - 1)]
    backward = [(i + 1, i) for i in range(members - 1)]
    chunks = range(len(NEXT_CHUNKS))

    packed = pack(info, block_mask, density)
    above = [lax.ppermute(packed[2 * c + 1], AX, forward) for c in chunks]
    below = [lax.ppermute(packed[2 * c], AX, backward) for c in chunks]

    atoms = jnp.concatenate([positions, charges[None]], axis=0)[None]
    for axis in reversed(AX):
        atoms = lax.all_gather(atoms, axis, axis=0, tiled=True)
    cell = orbital_cell[None]
    shifts = shift_values(info, atoms, cell)
    work = work_matrix(info, block_mask, shifts, density)

    back_next, back_prev, received = [], [], []
    for c in chunks:
        to_prev, to_next = partial_products(c, work, above[c], below[c])
        back_next.append(lax.ppermute(to_prev, AX, backward))
        back_prev.append(lax.ppermute(to_next, AX, forward))
        received += [above[c], below[c]]
    new_density, diagonal = own_products(info, block_mask, work, received, density.shape)
    shares = energy_shares(info, atoms, cell, diagonal)
    gathered = lax.all_to_all(shares, AX, 0, 0, tiled=True)
    energies = charges * jnp.sum(gathered, axis=0).reshape(-1)

    at_next, at_prev = side_products(work)
    partials = []
    for c in chunks:
        partials += [back_next[c], back_prev[c]]
    new_density = finish(info, block_mask, at_next, at_prev, partials, new_density)
    return new_density, energies


def solution(mesh):
    in_specs = (
        P(AX, None, None, None),
        P(AX, None),
        P(AX),
        P(),
        P(None, AX),
        P(AX),
    )
    out_specs = (P(AX, None, None, None), P(AX))
    return jax.shard_map(on_device, mesh=mesh, in_specs=in_specs, out_specs=out_specs, check_vma=False)
```
